1024 devices in a mesh: seq: 32 (over z), pipe: 8 (over y, core), dp: 4 (over x).
Axes of the slice: x: 4, y: 4, z: 32, core: 2. Of those that a mesh axis runs over, the one named last changes fastest.
Arguments:
- saved_queries: bfloat16 [8, 4, 4096, 2048], P('pipe', 'dp', None, 'seq'), may hold values from -8 to 8
- saved_keys: bfloat16 [8, 4, 4096, 512], P('pipe', 'dp', 'seq'), may hold values from -8 to 8
- saved_values: bfloat16 [8, 4, 4096, 512], P('pipe', 'dp', 'seq'), may hold values from -6 to 6
- output_grad: bfloat16 [8, 4, 4096, 2048], P('pipe', 'dp', 'seq'), may hold values from -6 to 6
- rel_bias: float32 [8, 32, 256], P('pipe', 'seq'), may hold values from -4 to 4
- key_tiles: int32 [8, 32, 32, 4], P('pipe', 'seq'), may hold values from 0 to 31, as said below
- live_count: int32 [8, 32, 32], P('pipe', 'seq'), may hold values from 1 to 4
Outputs:
- carried_query_gradient: bfloat16 [8, 4, 4096, 2048], P('pipe', 'dp', 'seq')
- key_grad: bfloat16 [8, 4, 4096, 512], P('pipe', 'dp', 'seq')
- value_grad: bfloat16 [8, 4, 4096, 512], P('pipe', 'dp', 'seq')
- bias_grad: float32 [8, 32, 256], P('pipe', 'seq', 'dp')
The draws below stay inside these ranges and needn't reach their ends.
Inputs may be any that keep to these rules, and one draw needn't show every extreme that they name: `key_tiles`: for each section, head and query tile i, slot 0 holds i, the first live_count slots name distinct key tiles no later than i, and the other slots hold i.
All inputs are finite; a program needn't handle non-finite values.
Results may differ from the reference program's by a relative error of at most 0.0085.
Values may be sent and summed in bfloat16 or wider, within the bound.
No kernel may reach another device: no remote copies, remote signals or barrier semaphores. Data moves between devices by JAX's collectives and lax.ppermute only.
A program may use at most 64 MiB of HBM per device.

```python
import jax
import jax.numpy as jnp
from jax import lax

HEADS = 32
KVH = 8
HD = 64
TILE = 128
BUCKET = 16
SLOTS = 4
BAND_MAX = 2
BAR_STEP = 4
SECTIONS = 8
REPLICAS = 4
TOKENS = 4096
NT = 32
REL = 256


def drawn_rows(key, heads_here, for_queries):
    shape = (SECTIONS, REPLICAS, TOKENS, heads_here * HD)
    salt = 11 if for_queries else 13
    return jnp.clip(jax.random.normal(jax.random.fold_in(key, salt), shape, jnp.float32), -6.0, 6.0)


def draw_saved_queries(key, part):
    return drawn_rows(key, HEADS, True).astype(jnp.bfloat16)


def draw_saved_keys(key, part):
    return drawn_rows(key, KVH, False).astype(jnp.bfloat16)


def mask_plan(key):
    plan_base = jax.random.fold_in(key, 101)
    band_size = jax.random.randint(jax.random.fold_in(plan_base, 1), (SECTIONS, HEADS), 1, BAND_MAX + 1)
    bar_size = jax.random.randint(jax.random.fold_in(plan_base, 2), (SECTIONS, HEADS), 0, SLOTS - band_size + 1)
    head_order = jax.vmap(lambda head_key: jax.random.permutation(head_key, HEADS))(jax.random.split(jax.random.fold_in(plan_base, 3), SECTIONS))
    chosen_head = head_order == 0
    band_size = jnp.where(chosen_head, BAND_MAX, band_size)
    bar_size = jnp.where(chosen_head, SLOTS - BAND_MAX, bar_size)
    tile_ids = jnp.arange(NT)[None, None, :]
    band_live = jnp.minimum(band_size[..., None], tile_ids + 1)
    below_band = tile_ids - band_live
    bar_live = jnp.where(below_band >= 0, jnp.minimum(bar_size[..., None], below_band // BAR_STEP + 1), 0)
    live_total = band_live + bar_live
    slot_ids = jnp.arange(SLOTS)[None, None, None, :]
    first_bar = (jnp.maximum(below_band, 0) // BAR_STEP * BAR_STEP)[..., None]
    bar_tile = first_bar - (slot_ids - band_live[..., None]) * BAR_STEP
    own_tile = tile_ids[..., None]
    tile_table = jnp.where(slot_ids < band_live[..., None], own_tile - slot_ids, jnp.where(slot_ids < live_total[..., None], bar_tile, own_tile + 0 * slot_ids))
    return (tile_table.astype(jnp.int32), live_total.astype(jnp.int32))


def draw_key_tiles(key, part):
    return mask_plan(key)[0]


def draw_live_count(key, part):
    return mask_plan(key)[1]


def shard_levels(rng, shape, cuts, smallest, largest):
    loudness = 1.0
    for dim, shards_of in cuts:
        steps = jax.random.uniform(jax.random.fold_in(jax.random.fold_in(rng, 6), dim), (shards_of,), jnp.float32, smallest / len(cuts), largest / len(cuts))
        loudness = loudness * jnp.repeat(jnp.exp(steps), shape[dim] // shards_of).reshape((-1,) + (1,) * (len(shape) - 1 - dim))
    return loudness


def gaussian(rng, shape, spread, reach, cuts=(), kind=jnp.bfloat16):
    drawn = jax.random.normal(rng, shape, jnp.float32) * spread
    if len(cuts) > 0:
        drawn = shard_levels(rng, shape, cuts, -0.22, 0.18) * drawn
    return jnp.clip(drawn, min=-reach, max=reach).astype(kind)


def setup_inputs(seed: int = 0) -> dict:
    keys = jax.random.split(jax.random.key(seed), 8)
    return {
        "saved_queries": draw_saved_queries(jax.random.fold_in(keys[7], 71), 0),
        "saved_keys": draw_saved_keys(jax.random.fold_in(keys[7], 71), 0),
        "saved_values": gaussian(keys[2], (SECTIONS, REPLICAS, TOKENS, KVH * HD), 1.0, 6.0, ((0, 8), (1, 4), (2, 32))),
        "output_grad": gaussian(keys[3], (SECTIONS, REPLICAS, TOKENS, HEADS * HD), 1.0, 6.0, ((0, 8), (1, 4), (2, 32))),
        "rel_bias": gaussian(keys[4], (SECTIONS, HEADS, REL), 1.0, 4.0, ((0, 8), (1, 32)), jnp.float32),
        "key_tiles": draw_key_tiles(jax.random.fold_in(keys[7], 71), 0),
        "live_count": draw_live_count(jax.random.fold_in(keys[7], 71), 0),
    }


neg_big = -1.0e30


def rounded(values_in):
    lowered = values_in.astype(jnp.bfloat16)
    return lax.optimization_barrier(lowered).astype(jnp.float32)


def head_terms(queries, key_rows, value_rows, grad_rows, relative_bias_row, tile_list, live_slots):
    seq_len = queries.shape[0]
    tiles_n = seq_len // TILE
    logit_scale = HD ** -0.5
    query_blocks = queries.reshape(tiles_n, TILE, HD).astype(jnp.float32)
    key_all = key_rows.reshape(tiles_n, TILE, HD).astype(jnp.float32)
    value_all = value_rows.reshape(tiles_n, TILE, HD).astype(jnp.float32)
    grad_tiles = grad_rows.reshape(tiles_n, TILE, HD).astype(jnp.float32)
    current_key_block = key_all[tile_list]
    value_tile = value_all[tile_list]
    tile_ids = jnp.arange(tiles_n, dtype=jnp.int32)
    row_ids = jnp.arange(TILE, dtype=jnp.int32)
    distance = (tile_ids[:, None] - tile_list)[:, :, None, None] * TILE + row_ids[:, None] - row_ids[None, :]
    live_mask = jnp.arange(SLOTS, dtype=jnp.int32)[None, :] < live_slots[:, None]
    allowed = live_mask[:, :, None, None] & (distance >= 0)
    distance_buckets = jnp.clip(distance // BUCKET, 0, REL - 1)
    attention_logits = logit_scale * jnp.einsum('wcq,wekq->weck', query_blocks, current_key_block) + relative_bias_row[distance_buckets]
    attention_logits = jnp.where(allowed, attention_logits, neg_big)
    row_max = jnp.max(attention_logits, axis=(1, 3))
    weights = jnp.where(allowed, jnp.exp(attention_logits - row_max[:, None, :, None]), 0.0)
    log_norm = row_max + jnp.log(jnp.sum(weights, axis=(1, 3)))
    probs = jnp.where(allowed, jnp.exp(attention_logits - log_norm[:, None, :, None]), 0.0)
    probs_low = rounded(probs)
    grad_prob = jnp.einsum('iac,ijbc->ijab', grad_tiles, value_tile)
    row_delta = jnp.sum(probs * grad_prob, axis=(1, 3))
    grad_score = probs * (grad_prob - row_delta[:, None, :, None])
    gradient_reduced = rounded(grad_score)
    carried_query_gradient = (logit_scale * jnp.einsum('oqyx,oqxv->oyv', gradient_reduced, current_key_block)).astype(jnp.bfloat16)
    scatter_lookup = (tile_list[:, :, None] == tile_ids[None, None, :]).astype(jnp.float32)
    key_contribution = logit_scale * jnp.einsum('uar,uags->rgs', scatter_lookup, jnp.einsum('mgqr,mqf->mgrf', gradient_reduced, query_blocks))
    value_term = jnp.einsum('ijk,ijbc->kbc', scatter_lookup, jnp.einsum('ijab,iac->ijbc', probs_low, grad_tiles))
    bias_term = jax.ops.segment_sum(grad_score.reshape(-1), distance_buckets.reshape(-1), num_segments=REL)
    return (carried_query_gradient.reshape(seq_len, HD), key_contribution.astype(jnp.bfloat16).reshape(seq_len, HD),
            value_term.astype(jnp.bfloat16).reshape(seq_len, HD), bias_term)


def reference(saved_queries, saved_keys, saved_values, output_grad, rel_bias, key_tiles, live_count):
    sections, replicas, seq_len = saved_queries.shape[0], saved_queries.shape[1], saved_queries.shape[2]
    group_size = HEADS // KVH
    zero_index = jnp.zeros((), jnp.int32)

    def head_job(flat_id):
        section = flat_id // (replicas * HEADS)
        replica = (flat_id // HEADS) % replicas
        head_id = flat_id % HEADS
        group_id = head_id // group_size
        queries = lax.dynamic_slice(saved_queries, (section, replica, zero_index, head_id * HD), (1, 1, seq_len, HD))[0, 0]
        key_rows = lax.dynamic_slice(saved_keys, (section, replica, zero_index, group_id * HD), (1, 1, seq_len, HD))[0, 0]
        value_rows = lax.dynamic_slice(saved_values, (section, replica, zero_index, group_id * HD), (1, 1, seq_len, HD))[0, 0]
        grad_rows = lax.dynamic_slice(output_grad, (section, replica, zero_index, head_id * HD), (1, 1, seq_len, HD))[0, 0]
        relative_bias_row = lax.dynamic_slice(rel_bias, (section, head_id, zero_index), (1, 1, REL))[0, 0]
        tile_list = lax.dynamic_slice(key_tiles, (section, head_id, zero_index, zero_index), (1, 1, NT, SLOTS))[0, 0]
        live_slots = lax.dynamic_slice(live_count, (section, head_id, zero_index), (1, 1, NT))[0, 0]
        return head_terms(queries, key_rows, value_rows, grad_rows, relative_bias_row, tile_list, live_slots)

    flat_ids = jnp.arange(sections * replicas * HEADS, dtype=jnp.int32)
    query_all, key_all, value_all, bias_all = lax.map(head_job, flat_ids)
    query_part = query_all.reshape(sections, replicas, HEADS, seq_len, HD).transpose(0, 1, 3, 2, 4)
    query_part = query_part.reshape(sections, replicas, seq_len, HEADS * HD)

    def group_sum(terms):
        summed = terms.astype(jnp.float32).reshape(sections, replicas, KVH, group_size, seq_len, HD).sum(3)
        summed = summed.astype(jnp.bfloat16).transpose(0, 1, 3, 2, 4)
        return summed.reshape(sections, replicas, seq_len, KVH * HD)

    def passed(parts):
        return jnp.concatenate([parts[1:], jnp.zeros_like(parts[:1])], axis=0)

    bias_grad = bias_all.reshape(sections, replicas, HEADS, REL).sum(1)
    return passed(query_part), passed(group_sum(key_all)), passed(group_sum(value_all)), bias_grad
```

```python
import jax
import jax.numpy as jnp
from jax import lax
from jax.experimental import pallas as pl
from jax.experimental.pallas import tpu as pltpu
from jax.sharding import PartitionSpec as P

HEADS = 32
KVH = 8
HD = 64
TILE = 128
BUCKET = 16
SLOTS = 4
GROUP = HEADS // KVH
QUART = TILE // GROUP
PACK = HD + QUART

neg_big = -1e30
log2_e = 1.4426950408889634
low = jnp.bfloat16
wide = jnp.float32

in_vmem = pl.BlockSpec(memory_space=pltpu.VMEM)
in_smem = pl.BlockSpec(memory_space=pltpu.SMEM)


def params(mib):
    return pltpu.CompilerParams(vmem_limit_bytes=mib << 20)


def pack_kernel(grad_ref, key_ref, value_ref, out_ref):
    for pair in range(HEADS // 2):
        turned = grad_ref[:, pair * 2 * HD : (pair + 1) * 2 * HD].T
        out_ref[2 * pair, 0:HD, :] = turned[0:HD]
        out_ref[2 * pair + 1, 0:HD, :] = turned[HD : 2 * HD]
    for g in range(KVH):
        both = jnp.concatenate(
            [key_ref[:, g * HD : (g + 1) * HD], value_ref[:, g * HD : (g + 1) * HD]], axis=1
        )
        for j in range(GROUP):
            out_ref[g * GROUP + j, HD:PACK, :] = both[j * QUART : (j + 1) * QUART]


def unpack_kernel(in_ref, query_ref, key_ref, value_ref):
    for pair in range(HEADS // 2):
        both = jnp.concatenate([in_ref[2 * pair, 0:HD, :], in_ref[2 * pair + 1, 0:HD, :]], axis=0)
        query_ref[:, pair * 2 * HD : (pair + 1) * 2 * HD] = both.T
    for pair in range(KVH // 2):
        sides = []
        for g in (2 * pair, 2 * pair + 1):
            sides.append(
                jnp.concatenate(
                    [in_ref[g * GROUP + j, HD:PACK, :] for j in range(GROUP)], axis=0
                )
            )
        at = slice(pair * 2 * HD, (pair + 1) * 2 * HD)
        key_ref[:, at] = jnp.concatenate([s[:, 0:HD] for s in sides], axis=1)
        value_ref[:, at] = jnp.concatenate([s[:, HD : 2 * HD] for s in sides], axis=1)


def sum_kernel(in_ref, out_ref):
    total = in_ref[0].astype(wide)
    for head in range(1, GROUP):
        total = total + in_ref[head].astype(wide)
    out_ref[...] = total.astype(low)


def table_kernel(steps_ref, table_ref):
    tiles_n = steps_ref.shape[0]
    for apart in range(tiles_n):
        near = steps_ref[apart : apart + 1, :]
        far = steps_ref[max(apart - 1, 0) : max(apart - 1, 0) + 1, :]
        line = jnp.broadcast_to(jnp.concatenate([near, far], axis=1) * log2_e, (TILE, 2 * TILE))
        turned = pltpu.roll(line, 0, 1, stride=1, stride_axis=0)[:, 0:TILE]
        if apart == 0:
            key_at = lax.broadcasted_iota(jnp.int32, (TILE, TILE), 0)
            query_at = lax.broadcasted_iota(jnp.int32, (TILE, TILE), 1)
            turned = jnp.where(key_at > query_at, neg_big, turned)
        table_ref[apart] = turned
    table_ref[tiles_n] = jnp.full((TILE, TILE), neg_big, wide)


def main_kernel(
    tiles_ref, live_ref, query_ref, recv_ref, kv_ref, table_ref,
    dq_ref, dkv_ref, steps_ref,
    kv, kt, acc, bias_acc,
):
    tiles_n = recv_ref.shape[0]
    scale = HD ** (-0.5)

    def begin(b, carry):
        both = jnp.concatenate([kv_ref[j, b] for j in range(GROUP)], axis=0)
        kv[b] = both
        kt[b] = both.T[0:HD]
        acc[b] = jnp.zeros((TILE, 2 * HD), wide)
        bias_acc[b] = jnp.zeros((TILE, TILE), wide)
        return carry

    lax.fori_loop(0, tiles_n, begin, 0)
    bias_acc[tiles_n] = jnp.zeros((TILE, TILE), wide)
    blank = jnp.zeros((HD, TILE), low)

    def one_tile(i, carry):
        live = live_ref[i]
        tile_at = [tiles_ref[i, s] for s in range(SLOTS)]
        apart = [jnp.where(s < live, i - tile_at[s], tiles_n) for s in range(SLOTS)]
        query = query_ref[:, pl.ds(pl.multiple_of(i * TILE, TILE), TILE)]
        weights = jnp.concatenate(
            [
                jnp.concatenate([query, blank], axis=1),
                jnp.concatenate([blank, recv_ref[i, 0:HD, :]], axis=1),
            ],
            axis=0,
        )
        keys = jnp.concatenate([kv[t] for t in tile_at], axis=0)
        both = jnp.dot(keys, weights, preferred_element_type=wide)
        bias = jnp.concatenate([table_ref[d] for d in apart], axis=0)
        logits = both[:, 0:TILE] * (scale * log2_e) + bias
        grad_prob = both[:, TILE : 2 * TILE]
        top = jnp.max(logits, axis=0, keepdims=True)
        raised = jnp.exp2(logits - top)
        probs = raised * (1.0 / jnp.sum(raised, axis=0, keepdims=True))
        delta = jnp.sum(probs * grad_prob, axis=0, keepdims=True)
        grad = probs * (grad_prob - delta)
        grad_low = grad.astype(low)
        terms = lax.dot_general(
            jnp.concatenate([grad_low, probs.astype(low)], axis=1),
            weights,
            (((1,), (1,)), ((), ())),
            preferred_element_type=wide,
        )
        keys_turned = jnp.concatenate([kt[t] for t in tile_at], axis=1)
        dq = jnp.dot(keys_turned, grad_low, preferred_element_type=wide)
        dq_ref[i] = (dq * scale).astype(low)
        for s in range(SLOTS):
            rows = slice(s * TILE, (s + 1) * TILE)
            acc[tile_at[s]] += terms[rows]
            bias_acc[apart[s]] += grad[rows]
        return carry

    lax.fori_loop(0, tiles_n, one_tile, 0)
    lane = lax.broadcasted_iota(jnp.int32, (TILE, 2 * HD), 1)
    sizes = jnp.where(lane < HD, scale, 1.0)
    blank_right = jnp.zeros((TILE, TILE), wide)
    in_bucket = lax.broadcasted_iota(jnp.int32, (BUCKET, 2 * TILE), 1) % BUCKET
    before = in_bucket < lax.broadcasted_iota(jnp.int32, (BUCKET, 2 * TILE), 0)

    def end(b, carry):
        terms = (acc[b] * sizes).astype(low)
        for j in range(GROUP):
            dkv_ref[j, b] = terms[j * QUART : (j + 1) * QUART]
        padded = jnp.concatenate([bias_acc[b], blank_right], axis=1)
        lined = padded[0:BUCKET]
        for step in range(1, TILE // BUCKET):
            rows = padded[step * BUCKET : (step + 1) * BUCKET]
            lined = lined + pltpu.roll(rows, 2 * TILE - step * BUCKET, 1)
        same = jnp.sum(jnp.where(before, 0.0, lined), axis=0, keepdims=True)
        less = jnp.sum(jnp.where(before, lined, 0.0), axis=0, keepdims=True)
        steps_ref[b] = same + pltpu.roll(less, 2 * TILE - BUCKET, 1)
        return carry

    lax.fori_loop(0, tiles_n, end, 0)


def make_table(bias_row, tiles_n):
    steps = jnp.repeat(bias_row.reshape(tiles_n, TILE // BUCKET), BUCKET, axis=1)
    return pl.pallas_call(
        table_kernel,
        out_shape=jax.ShapeDtypeStruct((tiles_n + 1, TILE, TILE), wide),
        in_specs=[in_vmem],
        out_specs=in_vmem,
        compiler_params=params(16),
    )(steps)


def head_grads(tile_list, live_slots, query, recv, kv_parts, table):
    tiles_n = recv.shape[0]
    return pl.pallas_call(
        main_kernel,
        out_shape=(
            jax.ShapeDtypeStruct((tiles_n, HD, TILE), low),
            jax.ShapeDtypeStruct((GROUP, tiles_n, QUART, 2 * HD), low),
            jax.ShapeDtypeStruct((tiles_n, 1, 2 * TILE), wide),
        ),
        in_specs=[in_smem, in_smem, in_vmem, in_vmem, in_vmem, in_vmem],
        out_specs=(in_vmem, in_vmem, in_vmem),
        scratch_shapes=[
            pltpu.VMEM((tiles_n, TILE, 2 * HD), low),
            pltpu.VMEM((tiles_n, HD, TILE), low),
            pltpu.VMEM((tiles_n, TILE, 2 * HD), wide),
            pltpu.VMEM((tiles_n + 1, TILE, TILE), wide),
        ],
        compiler_params=params(32),
    )(tile_list, live_slots, query, recv, kv_parts, table)


def bias_row_of(steps):
    near, far = steps[:, 0, 0:TILE], steps[:, 0, TILE : 2 * TILE]
    far = jnp.concatenate([far[1:], jnp.zeros_like(far[:1])], axis=0)
    tiles_n = steps.shape[0]
    return (near + far).reshape(1, tiles_n * (TILE // BUCKET), BUCKET).sum(2)


def per_device(
    saved_queries, saved_keys, saved_values, output_grad, rel_bias, key_tiles, live_count
):
    seq_n = lax.axis_size("seq")
    groups = [[g * GROUP + j for j in range(GROUP)] for g in range(seq_n // GROUP)]
    tiles_n = key_tiles.shape[2]
    packed = pl.pallas_call(
        pack_kernel,
        out_shape=jax.ShapeDtypeStruct((HEADS, PACK, TILE), low),
        in_specs=[in_vmem] * 3,
        out_specs=in_vmem,
        compiler_params=params(16),
    )(output_grad[0, 0], saved_keys[0, 0], saved_values[0, 0])
    recv = lax.all_to_all(packed, "seq", split_axis=0, concat_axis=0, tiled=True)
    kv_parts = lax.all_gather(recv[:, HD:PACK, :], "seq", axis=0, axis_index_groups=groups)
    table = make_table(rel_bias[0, 0], tiles_n)
    dq, dkv, steps = head_grads(
        key_tiles[0, 0], live_count[0, 0], saved_queries[0, 0].T, recv, kv_parts, table
    )
    bias_share = lax.psum_scatter(bias_row_of(steps), "dp", scatter_dimension=1, tiled=True)
    sections = lax.axis_size("pipe")
    back = [(p + 1, p) for p in range(sections - 1)]
    dq = lax.ppermute(dq, "pipe", back)
    terms = lax.all_to_all(
        dkv, "seq", split_axis=0, concat_axis=0, tiled=True, axis_index_groups=groups
    )
    summed = pl.pallas_call(
        sum_kernel,
        out_shape=jax.ShapeDtypeStruct((tiles_n, QUART, 2 * HD), low),
        in_specs=[in_vmem],
        out_specs=in_vmem,
        compiler_params=params(16),
    )(terms)
    summed = lax.ppermute(summed, "pipe", back)
    back_in = lax.all_to_all(
        jnp.concatenate([dq, summed], axis=1), "seq", split_axis=0, concat_axis=0, tiled=True
    )
    sent_query, sent_keys, sent_values = pl.pallas_call(
        unpack_kernel,
        out_shape=(
            jax.ShapeDtypeStruct((TILE, HEADS * HD), low),
            jax.ShapeDtypeStruct((TILE, KVH * HD), low),
            jax.ShapeDtypeStruct((TILE, KVH * HD), low),
        ),
        in_specs=[in_vmem],
        out_specs=(in_vmem,) * 3,
        compiler_params=params(16),
    )(back_in)
    return (
        sent_query[None, None],
        sent_keys[None, None],
        sent_values[None, None],
        bias_share[None],
    )


def solution(mesh):
    placed = (
        P("pipe", "dp", None, "seq"),
        P("pipe", "dp", "seq", None),
        P("pipe", "dp", "seq", None),
        P("pipe", "dp", "seq", None),
        P("pipe", "seq", None),
        P("pipe", "seq", None, None),
        P("pipe", "seq", None),
    )
    return jax.shard_map(
        per_device,
        mesh=mesh,
        in_specs=placed,
        out_specs=(
            P("pipe", "dp", "seq", None),
            P("pipe", "dp", "seq", None),
            P("pipe", "dp", "seq", None),
            P("pipe", "seq", "dp"),
        ),
        check_vma=False,
    )
```

```python
import jax
import jax.numpy as jnp
from jax import lax
from jax.experimental import pallas as pl
from jax.experimental.pallas import tpu as pltpu
from jax.sharding import PartitionSpec as P

HEADS = 32
KVH = 8
HD = 64
TILE = 128
BUCKET = 16
SLOTS = 4
GROUP = HEADS // KVH
QUART = TILE // GROUP
PACK = HD + QUART

neg_big = -1e30
log2_e = 1.4426950408889634
low = jnp.bfloat16
wide = jnp.float32

in_vmem = pl.BlockSpec(memory_space=pltpu.VMEM)
in_smem = pl.BlockSpec(memory_space=pltpu.SMEM)


def params(mib):
    return pltpu.CompilerParams(vmem_limit_bytes=mib << 20)


def pack_kernel(grad_hbm, key_hbm, value_hbm, out_ref, grad_ref, key_ref, value_ref, sems):
    copies = [
        pltpu.make_async_copy(source, held, sems.at[n])
        for n, (source, held) in enumerate(
            ((grad_hbm, grad_ref), (key_hbm, key_ref), (value_hbm, value_ref))
        )
    ]
    for copy in copies:
        copy.start()
    copies[0].wait()
    for pair in range(HEADS // 2):
        turned = grad_ref[:, pair * 2 * HD : (pair + 1) * 2 * HD].T
        out_ref[2 * pair, 0:HD, :] = turned[0:HD]
        out_ref[2 * pair + 1, 0:HD, :] = turned[HD : 2 * HD]
    copies[1].wait()
    copies[2].wait()
    for g in range(KVH):
        both = jnp.concatenate(
            [key_ref[:, g * HD : (g + 1) * HD], value_ref[:, g * HD : (g + 1) * HD]], axis=1
        )
        for j in range(GROUP):
            out_ref[g * GROUP + j, HD:PACK, :] = both[j * QUART : (j + 1) * QUART]


def unpack_kernel(in_ref, query_ref, key_ref, value_ref):
    for pair in range(HEADS // 2):
        both = jnp.concatenate([in_ref[2 * pair, 0:HD, :], in_ref[2 * pair + 1, 0:HD, :]], axis=0)
        query_ref[:, pair * 2 * HD : (pair + 1) * 2 * HD] = both.T
    for pair in range(KVH // 2):
        sides = []
        for g in (2 * pair, 2 * pair + 1):
            sides.append(
                jnp.concatenate(
                    [in_ref[g * GROUP + j, HD:PACK, :] for j in range(GROUP)], axis=0
                )
            )
        at = slice(pair * 2 * HD, (pair + 1) * 2 * HD)
        key_ref[:, at] = jnp.concatenate([s[:, 0:HD] for s in sides], axis=1)
        value_ref[:, at] = jnp.concatenate([s[:, HD : 2 * HD] for s in sides], axis=1)


def sum_kernel(query_ref, *refs):
    terms, out_ref = refs[:GROUP], refs[GROUP]
    out_ref[:, 0:HD, :] = query_ref[...]
    total = terms[0][...].astype(wide)
    for term in terms[1:]:
        total = total + term[...].astype(wide)
    out_ref[:, HD:PACK, :] = total.astype(low)


def table_kernel(steps_ref, table_ref):
    tiles_n = steps_ref.shape[0]
    for apart in range(tiles_n):
        near = steps_ref[apart : apart + 1, :]
        far = steps_ref[max(apart - 1, 0) : max(apart - 1, 0) + 1, :]
        line = jnp.broadcast_to(jnp.concatenate([near, far], axis=1) * log2_e, (TILE, 2 * TILE))
        turned = pltpu.roll(line, 0, 1, stride=1, stride_axis=0)[:, 0:TILE]
        if apart == 0:
            key_at = lax.broadcasted_iota(jnp.int32, (TILE, TILE), 0)
            query_at = lax.broadcasted_iota(jnp.int32, (TILE, TILE), 1)
            turned = jnp.where(key_at > query_at, neg_big, turned)
        table_ref[apart] = turned
    table_ref[tiles_n] = jnp.full((TILE, TILE), neg_big, wide)


def main_kernel(
    place_ref, tiles_ref, live_ref, query_ref, recv_ref, *refs,
):
    parts, table_ref, dq_ref = refs[: GROUP - 1], refs[GROUP - 1], refs[GROUP]
    outs, steps_ref = refs[GROUP + 1 : 2 * GROUP + 1], refs[2 * GROUP + 1]
    kv, kt, acc, bias_acc, even, odd = refs[2 * GROUP + 2 :]
    tiles_n = recv_ref.shape[0]
    scale = HD ** (-0.5)
    place = place_ref[0]

    def quarter(j):
        return pl.ds(pl.multiple_of(lax.rem(j, GROUP) * QUART, QUART), QUART)

    def begin(b, carry):
        kv[b, quarter(place), :] = recv_ref[b, HD:PACK, :]
        for d in range(1, GROUP):
            kv[b, quarter(place + GROUP - d), :] = parts[d - 1][b]
        kt[b] = kv[b].T[0:HD]
        bias_acc[b] = jnp.zeros((TILE, TILE), wide)
        return carry

    lax.fori_loop(0, tiles_n, begin, 0, unroll=8)
    bias_acc[tiles_n] = jnp.zeros((TILE, TILE), wide)
    blank = jnp.zeros((HD, TILE), low)
    slots = [slice(s * TILE, (s + 1) * TILE) for s in range(SLOTS)]

    def weights_of(i):
        query = query_ref[:, pl.ds(pl.multiple_of(i * TILE, TILE), TILE)]
        return jnp.concatenate(
            [
                jnp.concatenate([query, blank], axis=1),
                jnp.concatenate([blank, recv_ref[i, 0:HD, :]], axis=1),
            ],
            axis=0,
        )

    def products(i):
        keys = jnp.concatenate([kv[tiles_ref[i, s]] for s in range(SLOTS)], axis=0)
        return jnp.dot(keys, weights_of(i), preferred_element_type=wide)

    def rest(i, both):
        live = live_ref[i]
        tile_at = [tiles_ref[i, s] for s in range(SLOTS)]
        apart = [jnp.where(s < live, i - tile_at[s], tiles_n) for s in range(SLOTS)]
        logits = [
            both[rows, 0:TILE] * (scale * log2_e) + table_ref[d] for rows, d in zip(slots, apart)
        ]
        most = jnp.maximum(jnp.maximum(logits[0], logits[1]), jnp.maximum(logits[2], logits[3]))
        top = jnp.max(most, axis=0, keepdims=True)
        raised, total, weighed = [], 0.0, 0.0
        for rows, logit in zip(slots, logits):
            raised.append(jnp.exp2(logit - top))
            total = total + raised[-1]
            weighed = weighed + raised[-1] * both[rows, TILE : 2 * TILE]
        inverse = 1.0 / jnp.sum(total, axis=0, keepdims=True)
        delta = jnp.sum(weighed, axis=0, keepdims=True) * inverse
        probs_low, grad_low = [], []
        for s in range(SLOTS):
            probs = raised[s] * inverse
            grad = probs * (both[slots[s], TILE : 2 * TILE] - delta)
            bias_acc[apart[s]] += grad
            probs_low.append(probs.astype(low))
            grad_low.append(grad.astype(low))
        grad_low = jnp.concatenate(grad_low, axis=0)
        probs_low = jnp.concatenate(probs_low, axis=0)
        terms = lax.dot_general(
            jnp.concatenate([grad_low, probs_low], axis=1),
            weights_of(i),
            (((1,), (1,)), ((), ())),
            preferred_element_type=wide,
        )
        keys_turned = jnp.concatenate([kt[t] for t in tile_at], axis=1)
        dq = jnp.dot(keys_turned, grad_low, preferred_element_type=wide)
        dq_ref[i] = (dq * scale).astype(low)
        acc[i] = terms[slots[0]]
        for s in range(1, SLOTS):
            acc[tile_at[s]] += terms[slots[s]]

    even[...] = products(0)

    def two_tiles(n, carry):
        i = 2 * n
        odd[...] = products(i + 1)
        rest(i, even)
        even[...] = products(jnp.minimum(i + 2, tiles_n - 1))
        rest(i + 1, odd)
        return carry

    lax.fori_loop(0, tiles_n // 2, two_tiles, 0, unroll=2)
    lane = lax.broadcasted_iota(jnp.int32, (QUART, 2 * HD), 1)
    sizes = jnp.where(lane < HD, scale, 1.0)
    blank_right = jnp.zeros((TILE, TILE), wide)
    in_bucket = lax.broadcasted_iota(jnp.int32, (BUCKET, 2 * TILE), 1) % BUCKET
    before = in_bucket < lax.broadcasted_iota(jnp.int32, (BUCKET, 2 * TILE), 0)

    def end(b, carry):
        for d in range(GROUP):
            outs[d][b] = (acc[b, quarter(place + d), :] * sizes).astype(low)
        padded = jnp.concatenate([bias_acc[b], blank_right], axis=1)
        lined = padded[0:BUCKET]
        for step in range(1, TILE // BUCKET):
            rows = padded[step * BUCKET : (step + 1) * BUCKET]
            lined = lined + pltpu.roll(rows, 2 * TILE - step * BUCKET, 1)
        same = jnp.sum(jnp.where(before, 0.0, lined), axis=0, keepdims=True)
        less = jnp.sum(jnp.where(before, lined, 0.0), axis=0, keepdims=True)
        steps_ref[b] = same + pltpu.roll(less, 2 * TILE - BUCKET, 1)
        return carry

    lax.fori_loop(0, tiles_n, end, 0, unroll=8)


def make_table(bias_row, tiles_n):
    steps = jnp.repeat(bias_row.reshape(tiles_n, TILE // BUCKET), BUCKET, axis=1)
    return pl.pallas_call(
        table_kernel,
        out_shape=jax.ShapeDtypeStruct((tiles_n + 1, TILE, TILE), wide),
        in_specs=[in_vmem],
        out_specs=in_vmem,
        compiler_params=params(16),
    )(steps)


def head_grads(place, tile_list, live_slots, query, recv, parts, table):
    tiles_n = recv.shape[0]
    share = jax.ShapeDtypeStruct((tiles_n, QUART, 2 * HD), low)
    return pl.pallas_call(
        main_kernel,
        out_shape=(
            jax.ShapeDtypeStruct((tiles_n, HD, TILE), low),
            *[share] * GROUP,
            jax.ShapeDtypeStruct((tiles_n, 1, 2 * TILE), wide),
        ),
        in_specs=[in_smem] * 3 + [in_vmem] * (GROUP + 2),
        out_specs=(in_vmem,) * (GROUP + 2),
        scratch_shapes=[
            pltpu.VMEM((tiles_n, TILE, 2 * HD), low),
            pltpu.VMEM((tiles_n, HD, TILE), low),
            pltpu.VMEM((tiles_n, TILE, 2 * HD), wide),
            pltpu.VMEM((tiles_n + 1, TILE, TILE), wide),
            pltpu.VMEM((SLOTS * TILE, 2 * TILE), wide),
            pltpu.VMEM((SLOTS * TILE, 2 * TILE), wide),
        ],
        compiler_params=params(32),
    )(place, tile_list, live_slots, query, recv, *parts, table)


def bias_row_of(steps):
    near, far = steps[:, 0, 0:TILE], steps[:, 0, TILE : 2 * TILE]
    far = jnp.concatenate([far[1:], jnp.zeros_like(far[:1])], axis=0)
    tiles_n = steps.shape[0]
    return (near + far).reshape(1, tiles_n * (TILE // BUCKET), BUCKET).sum(2)


def per_device(
    saved_queries, saved_keys, saved_values, output_grad, rel_bias, key_tiles, live_count
):
    seq_n, sections = lax.axis_size("seq"), lax.axis_size("pipe")
    tiles_n = key_tiles.shape[2]

    def passed_on(d):
        return [
            (g * GROUP + j, g * GROUP + (j + d) % GROUP)
            for g in range(seq_n // GROUP)
            for j in range(GROUP)
        ]

    packed = pl.pallas_call(
        pack_kernel,
        out_shape=jax.ShapeDtypeStruct((HEADS, PACK, TILE), low),
        in_specs=[pl.BlockSpec(memory_space=pltpu.HBM)] * 3,
        out_specs=in_vmem,
        scratch_shapes=[
            pltpu.VMEM((TILE, HEADS * HD), low),
            pltpu.VMEM((TILE, KVH * HD), low),
            pltpu.VMEM((TILE, KVH * HD), low),
            pltpu.SemaphoreType.DMA((3,)),
        ],
        compiler_params=params(16),
    )(output_grad[0, 0], saved_keys[0, 0], saved_values[0, 0])
    recv = lax.all_to_all(packed, "seq", split_axis=0, concat_axis=0, tiled=True)
    table = make_table(rel_bias[0, 0], tiles_n)
    own, table = lax.optimization_barrier((recv[:, HD:PACK, :], table))
    parts = [lax.ppermute(own, "seq", passed_on(d)) for d in range(1, GROUP)]
    place = (lax.axis_index("seq") % GROUP).astype(jnp.int32).reshape(1)
    dq, *terms, steps = head_grads(
        place, key_tiles[0, 0], live_count[0, 0], saved_queries[0, 0].T, recv, parts, table
    )
    bias_share = lax.psum_scatter(bias_row_of(steps), "dp", scatter_dimension=1, tiled=True)

    def moved(x, d):
        pairs = [
            (a * sections + p + 1, b * sections + p)
            for a, b in passed_on(d)
            for p in range(sections - 1)
        ]
        return lax.ppermute(x, ("seq", "pipe"), pairs)

    terms = [moved(x, d) for d, x in enumerate(terms)]
    dq = moved(dq, 0)
    packed = pl.pallas_call(
        sum_kernel,
        out_shape=jax.ShapeDtypeStruct((tiles_n, PACK, TILE), low),
        in_specs=[in_vmem] * (GROUP + 1),
        out_specs=in_vmem,
        compiler_params=params(16),
    )(dq, *terms)
    back_in = lax.all_to_all(packed, "seq", split_axis=0, concat_axis=0, tiled=True)
    sent_query, sent_keys, sent_values = pl.pallas_call(
        unpack_kernel,
        out_shape=(
            jax.ShapeDtypeStruct((TILE, HEADS * HD), low),
            jax.ShapeDtypeStruct((TILE, KVH * HD), low),
            jax.ShapeDtypeStruct((TILE, KVH * HD), low),
        ),
        in_specs=[in_vmem],
        out_specs=(in_vmem,) * 3,
        compiler_params=params(16),
    )(back_in)
    return (
        sent_query[None, None],
        sent_keys[None, None],
        sent_values[None, None],
        bias_share[None],
    )


def solution(mesh):
    placed = (
        P("pipe", "dp", None, "seq"),
        P("pipe", "dp", "seq", None),
        P("pipe", "dp", "seq", None),
        P("pipe", "dp", "seq", None),
        P("pipe", "seq", None),
        P("pipe", "seq", None, None),
        P("pipe", "seq", None),
    )
    return jax.shard_map(
        per_device,
        mesh=mesh,
        in_specs=placed,
        out_specs=(
            P("pipe", "dp", "seq", None),
            P("pipe", "dp", "seq", None),
            P("pipe", "dp", "seq", None),
            P("pipe", "seq", "dp"),
        ),
        check_vma=False,
    )
```

```python
import jax
import jax.numpy as jnp
from jax import lax
from jax.experimental import pallas as pl
from jax.experimental.pallas import tpu as pltpu
from jax.sharding import PartitionSpec as P

HEADS = 32
KVH = 8
HD = 64
TILE = 128
BUCKET = 16
SLOTS = 4
GROUP = HEADS // KVH
QUART = TILE // GROUP
PACK = HD + QUART

neg_big = -1e30
log2_e = 1.4426950408889634
low = jnp.bfloat16
wide = jnp.float32

in_vmem = pl.BlockSpec(memory_space=pltpu.VMEM)
in_smem = pl.BlockSpec(memory_space=pltpu.SMEM)


def params(mib):
    return pltpu.CompilerParams(vmem_limit_bytes=mib << 20)


def pack_kernel(grad_hbm, key_hbm, value_hbm, out_ref, grad_ref, key_ref, value_ref, sems):
    copies = [
        pltpu.make_async_copy(source, held, sems.at[n])
        for n, (source, held) in enumerate(
            ((grad_hbm, grad_ref), (key_hbm, key_ref), (value_hbm, value_ref))
        )
    ]
    for copy in copies:
        copy.start()
    copies[0].wait()
    for pair in range(HEADS // 2):
        turned = grad_ref[:, pair * 2 * HD : (pair + 1) * 2 * HD].T
        out_ref[2 * pair, 0:HD, :] = turned[0:HD]
        out_ref[2 * pair + 1, 0:HD, :] = turned[HD : 2 * HD]
    copies[1].wait()
    copies[2].wait()
    for g in range(KVH):
        both = jnp.concatenate(
            [key_ref[:, g * HD : (g + 1) * HD], value_ref[:, g * HD : (g + 1) * HD]], axis=1
        )
        for j in range(GROUP):
            out_ref[g * GROUP + j, HD:PACK, :] = both[j * QUART : (j + 1) * QUART]


def unpack_kernel(in_ref, query_ref, key_ref, value_ref):
    for pair in range(HEADS // 2):
        both = jnp.concatenate([in_ref[2 * pair, 0:HD, :], in_ref[2 * pair + 1, 0:HD, :]], axis=0)
        query_ref[:, pair * 2 * HD : (pair + 1) * 2 * HD] = both.T
    for pair in range(KVH // 2):
        sides = []
        for g in (2 * pair, 2 * pair + 1):
            sides.append(
                jnp.concatenate(
                    [in_ref[g * GROUP + j, HD:PACK, :] for j in range(GROUP)], axis=0
                )
            )
        at = slice(pair * 2 * HD, (pair + 1) * 2 * HD)
        key_ref[:, at] = jnp.concatenate([s[:, 0:HD] for s in sides], axis=1)
        value_ref[:, at] = jnp.concatenate([s[:, HD : 2 * HD] for s in sides], axis=1)


def sum_kernel(own_ref, *refs):
    terms, out_ref = refs[:-1], refs[-1]
    out_ref[:, 0:HD, :] = own_ref[:, 0:HD, :]
    total = own_ref[:, HD:PACK, :].astype(wide)
    for term in terms:
        total = total + term[...].astype(wide)
    out_ref[:, HD:PACK, :] = total.astype(low)


def table_kernel(steps_ref, table_ref):
    tiles_n = steps_ref.shape[0]
    for apart in range(tiles_n):
        near = steps_ref[apart : apart + 1, :]
        far = steps_ref[max(apart - 1, 0) : max(apart - 1, 0) + 1, :]
        line = jnp.broadcast_to(jnp.concatenate([near, far], axis=1) * log2_e, (TILE, 2 * TILE))
        turned = pltpu.roll(line, 0, 1, stride=1, stride_axis=0)[:, 0:TILE]
        if apart == 0:
            key_at = lax.broadcasted_iota(jnp.int32, (TILE, TILE), 0)
            query_at = lax.broadcasted_iota(jnp.int32, (TILE, TILE), 1)
            turned = jnp.where(key_at > query_at, neg_big, turned)
        table_ref[apart] = turned
    table_ref[tiles_n] = jnp.full((TILE, TILE), neg_big, wide)


def main_kernel(
    place_ref, tiles_ref, live_ref, query_ref, recv_ref, *refs,
):
    parts, table_ref, own_ref = refs[: GROUP - 1], refs[GROUP - 1], refs[GROUP]
    outs, steps_ref = refs[GROUP + 1 : 2 * GROUP], refs[2 * GROUP]
    kv, kt, acc, bias_acc, even, odd = refs[2 * GROUP + 1 :]
    tiles_n = recv_ref.shape[0]
    scale = HD ** (-0.5)
    place = place_ref[0]

    def quarter(j):
        return pl.ds(pl.multiple_of(lax.rem(j, GROUP) * QUART, QUART), QUART)

    def begin(b, carry):
        kv[b, quarter(place), :] = recv_ref[b, HD:PACK, :]
        for d in range(1, GROUP):
            kv[b, quarter(place + GROUP - d), :] = parts[d - 1][b]
        kt[b] = kv[b].T[0:HD]
        bias_acc[b] = jnp.zeros((TILE, TILE), wide)
        return carry

    lax.fori_loop(0, tiles_n, begin, 0, unroll=8)
    bias_acc[tiles_n] = jnp.zeros((TILE, TILE), wide)
    blank = jnp.zeros((HD, TILE), low)
    slots = [slice(s * TILE, (s + 1) * TILE) for s in range(SLOTS)]

    def weights_of(i):
        query = query_ref[:, pl.ds(pl.multiple_of(i * TILE, TILE), TILE)]
        return jnp.concatenate(
            [
                jnp.concatenate([query, blank], axis=1),
                jnp.concatenate([blank, recv_ref[i, 0:HD, :]], axis=1),
            ],
            axis=0,
        )

    def products(i):
        keys = jnp.concatenate([kv[tiles_ref[i, s]] for s in range(SLOTS)], axis=0)
        return jnp.dot(keys, weights_of(i), preferred_element_type=wide)

    def rest(i, both):
        live = live_ref[i]
        tile_at = [tiles_ref[i, s] for s in range(SLOTS)]
        apart = [jnp.where(s < live, i - tile_at[s], tiles_n) for s in range(SLOTS)]
        logits = [
            both[rows, 0:TILE] * (scale * log2_e) + table_ref[d] for rows, d in zip(slots, apart)
        ]
        most = jnp.maximum(jnp.maximum(logits[0], logits[1]), jnp.maximum(logits[2], logits[3]))
        top = jnp.max(most, axis=0, keepdims=True)
        raised, total, weighed = [], 0.0, 0.0
        for rows, logit in zip(slots, logits):
            raised.append(jnp.exp2(logit - top))
            total = total + raised[-1]
            weighed = weighed + raised[-1] * both[rows, TILE : 2 * TILE]
        inverse = 1.0 / jnp.sum(total, axis=0, keepdims=True)
        delta = jnp.sum(weighed, axis=0, keepdims=True) * inverse
        probs_low, grad_low = [], []
        for s in range(SLOTS):
            probs = raised[s] * inverse
            grad = probs * (both[slots[s], TILE : 2 * TILE] - delta)
            bias_acc[apart[s]] += grad
            probs_low.append(probs.astype(low))
            grad_low.append(grad.astype(low))
        grad_low = jnp.concatenate(grad_low, axis=0)
        probs_low = jnp.concatenate(probs_low, axis=0)
        terms = lax.dot_general(
            jnp.concatenate([grad_low, probs_low], axis=1),
            weights_of(i),
            (((1,), (1,)), ((), ())),
            preferred_element_type=wide,
        )
        keys_turned = jnp.concatenate([kt[t] for t in tile_at], axis=1)
        dq = jnp.dot(keys_turned, grad_low, preferred_element_type=wide)
        own_ref[i, 0:HD, :] = (dq * scale).astype(low)
        acc[i] = terms[slots[0]]
        for s in range(1, SLOTS):
            acc[tile_at[s]] += terms[slots[s]]

    even[...] = products(0)

    def two_tiles(n, carry):
        i = 2 * n
        odd[...] = products(i + 1)
        rest(i, even)
        even[...] = products(jnp.minimum(i + 2, tiles_n - 1))
        rest(i + 1, odd)
        return carry

    lax.fori_loop(0, tiles_n // 2, two_tiles, 0, unroll=4)
    lane = lax.broadcasted_iota(jnp.int32, (QUART, 2 * HD), 1)
    sizes = jnp.where(lane < HD, scale, 1.0)
    blank_right = jnp.zeros((TILE, TILE), wide)
    in_bucket = lax.broadcasted_iota(jnp.int32, (BUCKET, 2 * TILE), 1) % BUCKET
    before = in_bucket < lax.broadcasted_iota(jnp.int32, (BUCKET, 2 * TILE), 0)

    def end(b, carry):
        own_ref[b, HD:PACK, :] = (acc[b, quarter(place), :] * sizes).astype(low)
        for d in range(1, GROUP):
            outs[d - 1][b] = (acc[b, quarter(place + d), :] * sizes).astype(low)
        padded = jnp.concatenate([bias_acc[b], blank_right], axis=1)
        lined = padded[0:BUCKET]
        for step in range(1, TILE // BUCKET):
            rows = padded[step * BUCKET : (step + 1) * BUCKET]
            lined = lined + pltpu.roll(rows, 2 * TILE - step * BUCKET, 1)
        same = jnp.sum(jnp.where(before, 0.0, lined), axis=0, keepdims=True)
        less = jnp.sum(jnp.where(before, lined, 0.0), axis=0, keepdims=True)
        steps_ref[b] = same + pltpu.roll(less, 2 * TILE - BUCKET, 1)
        return carry

    lax.fori_loop(0, tiles_n, end, 0, unroll=8)


def make_table(bias_row, tiles_n):
    steps = jnp.repeat(bias_row.reshape(tiles_n, TILE // BUCKET), BUCKET, axis=1)
    return pl.pallas_call(
        table_kernel,
        out_shape=jax.ShapeDtypeStruct((tiles_n + 1, TILE, TILE), wide),
        in_specs=[in_vmem],
        out_specs=in_vmem,
        compiler_params=params(16),
    )(steps)


def head_grads(place, tile_list, live_slots, query, recv, parts, table):
    tiles_n = recv.shape[0]
    share = jax.ShapeDtypeStruct((tiles_n, QUART, 2 * HD), low)
    return pl.pallas_call(
        main_kernel,
        out_shape=(
            jax.ShapeDtypeStruct((tiles_n, PACK, TILE), low),
            *[share] * (GROUP - 1),
            jax.ShapeDtypeStruct((tiles_n, 1, 2 * TILE), wide),
        ),
        in_specs=[in_smem] * 3 + [in_vmem] * (GROUP + 2),
        out_specs=(in_vmem,) * (GROUP + 1),
        scratch_shapes=[
            pltpu.VMEM((tiles_n, TILE, 2 * HD), low),
            pltpu.VMEM((tiles_n, HD, TILE), low),
            pltpu.VMEM((tiles_n, TILE, 2 * HD), wide),
            pltpu.VMEM((tiles_n + 1, TILE, TILE), wide),
            pltpu.VMEM((SLOTS * TILE, 2 * TILE), wide),
            pltpu.VMEM((SLOTS * TILE, 2 * TILE), wide),
        ],
        compiler_params=params(32),
    )(place, tile_list, live_slots, query, recv, *parts, table)


def bias_row_of(steps):
    near, far = steps[:, 0, 0:TILE], steps[:, 0, TILE : 2 * TILE]
    far = jnp.concatenate([far[1:], jnp.zeros_like(far[:1])], axis=0)
    tiles_n = steps.shape[0]
    return (near + far).reshape(1, tiles_n * (TILE // BUCKET), BUCKET).sum(2)


def per_device(
    saved_queries, saved_keys, saved_values, output_grad, rel_bias, key_tiles, live_count
):
    seq_n, sections = lax.axis_size("seq"), lax.axis_size("pipe")
    tiles_n = key_tiles.shape[2]

    def passed_on(d):
        return [
            (g * GROUP + j, g * GROUP + (j + d) % GROUP)
            for g in range(seq_n // GROUP)
            for j in range(GROUP)
        ]

    def held(x):
        return pltpu.with_memory_space_constraint(x, pltpu.HBM)

    packed = pl.pallas_call(
        pack_kernel,
        out_shape=jax.ShapeDtypeStruct((HEADS, PACK, TILE), low),
        in_specs=[pl.BlockSpec(memory_space=pltpu.HBM)] * 3,
        out_specs=in_vmem,
        scratch_shapes=[
            pltpu.VMEM((TILE, HEADS * HD), low),
            pltpu.VMEM((TILE, KVH * HD), low),
            pltpu.VMEM((TILE, KVH * HD), low),
            pltpu.SemaphoreType.DMA((3,)),
        ],
        compiler_params=params(16),
    )(*[held(x[0, 0]) for x in (output_grad, saved_keys, saved_values)])
    recv = lax.all_to_all(packed, "seq", split_axis=0, concat_axis=0, tiled=True)
    table = make_table(rel_bias[0, 0], tiles_n)
    quarters, table = lax.optimization_barrier((recv[:, HD:PACK, :], table))
    parts = [lax.ppermute(quarters, "seq", passed_on(d)) for d in range(1, GROUP)]
    place = (lax.axis_index("seq") % GROUP).astype(jnp.int32).reshape(1)
    own, *terms, steps = head_grads(
        place, key_tiles[0, 0], live_count[0, 0], saved_queries[0, 0].T, recv, parts, table
    )
    bias_share = lax.psum_scatter(bias_row_of(steps), "dp", scatter_dimension=1, tiled=True)

    def moved(x, d):
        pairs = [
            (a * sections + p + 1, b * sections + p)
            for a, b in passed_on(d)
            for p in range(sections - 1)
        ]
        return lax.ppermute(x, ("seq", "pipe"), pairs)

    terms = [moved(x, d) for d, x in enumerate(terms, 1)]
    own = moved(own, 0)
    packed = pl.pallas_call(
        sum_kernel,
        out_shape=jax.ShapeDtypeStruct((tiles_n, PACK, TILE), low),
        in_specs=[in_vmem] * GROUP,
        out_specs=in_vmem,
        compiler_params=params(16),
    )(own, *terms)
    back_in = lax.all_to_all(packed, "seq", split_axis=0, concat_axis=0, tiled=True)
    sent_query, sent_keys, sent_values = pl.pallas_call(
        unpack_kernel,
        out_shape=(
            jax.ShapeDtypeStruct((TILE, HEADS * HD), low),
            jax.ShapeDtypeStruct((TILE, KVH * HD), low),
            jax.ShapeDtypeStruct((TILE, KVH * HD), low),
        ),
        in_specs=[in_vmem],
        out_specs=(in_vmem,) * 3,
        compiler_params=params(16),
    )(back_in)
    return (
        sent_query[None, None],
        sent_keys[None, None],
        sent_values[None, None],
        bias_share[None],
    )


def solution(mesh):
    placed = (
        P("pipe", "dp", None, "seq"),
        P("pipe", "dp", "seq", None),
        P("pipe", "dp", "seq", None),
        P("pipe", "dp", "seq", None),
        P("pipe", "seq", None),
        P("pipe", "seq", None, None),
        P("pipe", "seq", None),
    )
    return jax.shard_map(
        per_device,
        mesh=mesh,
        in_specs=placed,
        out_specs=(
            P("pipe", "dp", "seq", None),
            P("pipe", "dp", "seq", None),
            P("pipe", "dp", "seq", None),
            P("pipe", "seq", "dp"),
        ),
        check_vma=False,
    )
```

```python
import jax
import jax.numpy as jnp
from jax import lax
from jax.experimental import pallas as pl
from jax.experimental.pallas import tpu as pltpu
from jax.sharding import PartitionSpec as P

HEADS = 32
KVH = 8
HD = 64
TILE = 128
BUCKET = 16
SLOTS = 4
GROUP = HEADS // KVH
QUART = TILE // GROUP
PACK = HD + QUART

neg_big = -1e30
log2_e = 1.4426950408889634
low = jnp.bfloat16
wide = jnp.float32

in_vmem = pl.BlockSpec(memory_space=pltpu.VMEM)
in_smem = pl.BlockSpec(memory_space=pltpu.SMEM)


def params(mib):
    return pltpu.CompilerParams(vmem_limit_bytes=mib << 20)


def pack_kernel(grad_hbm, key_hbm, value_hbm, out_ref, grad_ref, key_ref, value_ref, sems):
    copies = [
        pltpu.make_async_copy(source, held, sems.at[n])
        for n, (source, held) in enumerate(
            ((grad_hbm, grad_ref), (key_hbm, key_ref), (value_hbm, value_ref))
        )
    ]
    for copy in copies:
        copy.start()
    copies[0].wait()
    for pair in range(HEADS // 2):
        turned = grad_ref[:, pair * 2 * HD : (pair + 1) * 2 * HD].T
        out_ref[2 * pair, 0:HD, :] = turned[0:HD]
        out_ref[2 * pair + 1, 0:HD, :] = turned[HD : 2 * HD]
    copies[1].wait()
    copies[2].wait()
    for g in range(KVH):
        both = jnp.concatenate(
            [key_ref[:, g * HD : (g + 1) * HD], value_ref[:, g * HD : (g + 1) * HD]], axis=1
        )
        for j in range(GROUP):
            out_ref[g * GROUP + j, HD:PACK, :] = both[j * QUART : (j + 1) * QUART]


def unpack_kernel(in_ref, query_ref, key_ref, value_ref):
    for pair in range(HEADS // 2):
        both = jnp.concatenate([in_ref[2 * pair, 0:HD, :], in_ref[2 * pair + 1, 0:HD, :]], axis=0)
        query_ref[:, pair * 2 * HD : (pair + 1) * 2 * HD] = both.T
    for pair in range(KVH // 2):
        sides = []
        for g in (2 * pair, 2 * pair + 1):
            sides.append(
                jnp.concatenate(
                    [in_ref[g * GROUP + j, HD:PACK, :] for j in range(GROUP)], axis=0
                )
            )
        at = slice(pair * 2 * HD, (pair + 1) * 2 * HD)
        key_ref[:, at] = jnp.concatenate([s[:, 0:HD] for s in sides], axis=1)
        value_ref[:, at] = jnp.concatenate([s[:, HD : 2 * HD] for s in sides], axis=1)


def sum_kernel(own_ref, *refs):
    terms, out_ref = refs[:-1], refs[-1]
    out_ref[:, 0:HD, :] = own_ref[:, 0:HD, :]
    total = own_ref[:, HD:PACK, :].astype(wide)
    for term in terms:
        total = total + term[...].astype(wide)
    out_ref[:, HD:PACK, :] = total.astype(low)


def table_kernel(steps_ref, table_ref):
    tiles_n = steps_ref.shape[0]
    for apart in range(tiles_n):
        near = steps_ref[apart : apart + 1, :]
        far = steps_ref[max(apart - 1, 0) : max(apart - 1, 0) + 1, :]
        line = jnp.broadcast_to(jnp.concatenate([near, far], axis=1) * log2_e, (TILE, 2 * TILE))
        turned = pltpu.roll(line, 0, 1, stride=1, stride_axis=0)[:, 0:TILE]
        if apart == 0:
            key_at = lax.broadcasted_iota(jnp.int32, (TILE, TILE), 0)
            query_at = lax.broadcasted_iota(jnp.int32, (TILE, TILE), 1)
            turned = jnp.where(key_at > query_at, neg_big, turned)
        table_ref[apart] = turned
    table_ref[tiles_n] = jnp.full((TILE, TILE), neg_big, wide)


def main_kernel(
    place_ref, tiles_ref, live_ref, query_ref, recv_ref, *refs,
):
    parts, table_ref, own_ref = refs[:GROUP], refs[GROUP], refs[GROUP + 1]
    outs, steps_ref = refs[GROUP + 2 : 2 * GROUP + 1], refs[2 * GROUP + 1]
    kv, kt, acc, bias_acc, even, odd = refs[2 * GROUP + 2 :]
    tiles_n = recv_ref.shape[0]
    scale = HD ** (-0.5)
    place = place_ref[0]

    def quarter(j):
        return pl.ds(pl.multiple_of(lax.rem(j, GROUP) * QUART, QUART), QUART)

    def begin(b, carry):
        across, below, above, passed = [part[b] for part in parts]
        kv[b, quarter(place), :] = recv_ref[b, HD:PACK, :]
        kv[b, quarter(place + 2), :] = across
        kv[b, quarter(place + 3), :] = jnp.where(place == 0, passed, below)
        kv[b, quarter(place + 1), :] = jnp.where(place == GROUP - 1, passed, above)
        kt[b] = kv[b].T[0:HD]
        bias_acc[b] = jnp.zeros((TILE, TILE), wide)
        return carry

    lax.fori_loop(0, tiles_n, begin, 0, unroll=8)
    bias_acc[tiles_n] = jnp.zeros((TILE, TILE), wide)
    blank = jnp.zeros((HD, TILE), low)
    slots = [slice(s * TILE, (s + 1) * TILE) for s in range(SLOTS)]

    def weights_of(i):
        query = query_ref[:, pl.ds(pl.multiple_of(i * TILE, TILE), TILE)]
        return jnp.concatenate(
            [
                jnp.concatenate([query, blank], axis=1),
                jnp.concatenate([blank, recv_ref[i, 0:HD, :]], axis=1),
            ],
            axis=0,
        )

    def products(i):
        keys = jnp.concatenate([kv[tiles_ref[i, s]] for s in range(SLOTS)], axis=0)
        return jnp.dot(keys, weights_of(i), preferred_element_type=wide)

    def rest(i, both):
        live = live_ref[i]
        tile_at = [tiles_ref[i, s] for s in range(SLOTS)]
        apart = [jnp.where(s < live, i - tile_at[s], tiles_n) for s in range(SLOTS)]
        logits = [
            both[rows, 0:TILE] * (scale * log2_e) + table_ref[d] for rows, d in zip(slots, apart)
        ]
        most = jnp.maximum(jnp.maximum(logits[0], logits[1]), jnp.maximum(logits[2], logits[3]))
        top = jnp.max(most, axis=0, keepdims=True)
        raised, total, weighed = [], 0.0, 0.0
        for rows, logit in zip(slots, logits):
            raised.append(jnp.exp2(logit - top))
            total = total + raised[-1]
            weighed = weighed + raised[-1] * both[rows, TILE : 2 * TILE]
        inverse = 1.0 / jnp.sum(total, axis=0, keepdims=True)
        delta = jnp.sum(weighed, axis=0, keepdims=True) * inverse
        probs_low, grad_low = [], []
        for s in range(SLOTS):
            probs = raised[s] * inverse
            grad = probs * (both[slots[s], TILE : 2 * TILE] - delta)
            bias_acc[apart[s]] += grad
            probs_low.append(probs.astype(low))
            grad_low.append(grad.astype(low))
        grad_low = jnp.concatenate(grad_low, axis=0)
        probs_low = jnp.concatenate(probs_low, axis=0)
        terms = lax.dot_general(
            jnp.concatenate([grad_low, probs_low], axis=1),
            weights_of(i),
            (((1,), (1,)), ((), ())),
            preferred_element_type=wide,
        )
        keys_turned = jnp.concatenate([kt[t] for t in tile_at], axis=1)
        dq = jnp.dot(keys_turned, grad_low, preferred_element_type=wide)
        own_ref[i, 0:HD, :] = (dq * scale).astype(low)
        acc[i] = terms[slots[0]]
        for s in range(1, SLOTS):
            acc[tile_at[s]] += terms[slots[s]]

    even[...] = products(0)

    def two_tiles(n, carry):
        i = 2 * n
        odd[...] = products(i + 1)
        rest(i, even)
        even[...] = products(jnp.minimum(i + 2, tiles_n - 1))
        rest(i + 1, odd)
        return carry

    lax.fori_loop(0, tiles_n // 2, two_tiles, 0, unroll=4)
    lane = lax.broadcasted_iota(jnp.int32, (QUART, 2 * HD), 1)
    sizes = jnp.where(lane < HD, scale, 1.0)
    blank_right = jnp.zeros((TILE, TILE), wide)
    in_bucket = lax.broadcasted_iota(jnp.int32, (BUCKET, 2 * TILE), 1) % BUCKET
    before = in_bucket < lax.broadcasted_iota(jnp.int32, (BUCKET, 2 * TILE), 0)

    def end(b, carry):
        own_ref[b, HD:PACK, :] = (acc[b, quarter(place), :] * sizes).astype(low)
        for d in range(1, GROUP):
            outs[d - 1][b] = (acc[b, quarter(place + d), :] * sizes).astype(low)
        padded = jnp.concatenate([bias_acc[b], blank_right], axis=1)
        lined = padded[0:BUCKET]
        for step in range(1, TILE // BUCKET):
            rows = padded[step * BUCKET : (step + 1) * BUCKET]
            lined = lined + pltpu.roll(rows, 2 * TILE - step * BUCKET, 1)
        same = jnp.sum(jnp.where(before, 0.0, lined), axis=0, keepdims=True)
        less = jnp.sum(jnp.where(before, lined, 0.0), axis=0, keepdims=True)
        steps_ref[b] = same + pltpu.roll(less, 2 * TILE - BUCKET, 1)
        return carry

    lax.fori_loop(0, tiles_n, end, 0, unroll=8)


def make_table(bias_row, tiles_n):
    steps = jnp.repeat(bias_row.reshape(tiles_n, TILE // BUCKET), BUCKET, axis=1)
    return pl.pallas_call(
        table_kernel,
        out_shape=jax.ShapeDtypeStruct((tiles_n + 1, TILE, TILE), wide),
        in_specs=[in_vmem],
        out_specs=in_vmem,
        compiler_params=params(16),
    )(steps)


def head_grads(place, tile_list, live_slots, query, recv, parts, table):
    tiles_n = recv.shape[0]
    share = jax.ShapeDtypeStruct((tiles_n, QUART, 2 * HD), low)
    return pl.pallas_call(
        main_kernel,
        out_shape=(
            jax.ShapeDtypeStruct((tiles_n, PACK, TILE), low),
            *[share] * (GROUP - 1),
            jax.ShapeDtypeStruct((tiles_n, 1, 2 * TILE), wide),
        ),
        in_specs=[in_smem] * 3 + [in_vmem] * (GROUP + 3),
        out_specs=(in_vmem,) * (GROUP + 1),
        scratch_shapes=[
            pltpu.VMEM((tiles_n, TILE, 2 * HD), low),
            pltpu.VMEM((tiles_n, HD, TILE), low),
            pltpu.VMEM((tiles_n, TILE, 2 * HD), wide),
            pltpu.VMEM((tiles_n + 1, TILE, TILE), wide),
            pltpu.VMEM((SLOTS * TILE, 2 * TILE), wide),
            pltpu.VMEM((SLOTS * TILE, 2 * TILE), wide),
        ],
        compiler_params=params(32),
    )(place, tile_list, live_slots, query, recv, *parts, table)


def bias_row_of(steps):
    near, far = steps[:, 0, 0:TILE], steps[:, 0, TILE : 2 * TILE]
    far = jnp.concatenate([far[1:], jnp.zeros_like(far[:1])], axis=0)
    tiles_n = steps.shape[0]
    return (near + far).reshape(1, tiles_n * (TILE // BUCKET), BUCKET).sum(2)


def per_device(
    saved_queries, saved_keys, saved_values, output_grad, rel_bias, key_tiles, live_count
):
    seq_n, sections = lax.axis_size("seq"), lax.axis_size("pipe")
    tiles_n = key_tiles.shape[2]

    def passed_on(d):
        return [
            (g * GROUP + j, g * GROUP + (j + d) % GROUP)
            for g in range(seq_n // GROUP)
            for j in range(GROUP)
        ]

    def held(x):
        return pltpu.with_memory_space_constraint(x, pltpu.HBM)

    packed = pl.pallas_call(
        pack_kernel,
        out_shape=jax.ShapeDtypeStruct((HEADS, PACK, TILE), low),
        in_specs=[pl.BlockSpec(memory_space=pltpu.HBM)] * 3,
        out_specs=in_vmem,
        scratch_shapes=[
            pltpu.VMEM((TILE, HEADS * HD), low),
            pltpu.VMEM((TILE, KVH * HD), low),
            pltpu.VMEM((TILE, KVH * HD), low),
            pltpu.SemaphoreType.DMA((3,)),
        ],
        compiler_params=params(16),
    )(*[held(x[0, 0]) for x in (output_grad, saved_keys, saved_values)])
    recv = lax.all_to_all(packed, "seq", split_axis=0, concat_axis=0, tiled=True)
    table = make_table(rel_bias[0, 0], tiles_n)
    quarters, table = lax.optimization_barrier((recv[:, HD:PACK, :], table))
    starts = range(0, seq_n, GROUP)

    def within(x, pairs):
        return lax.ppermute(x, "seq", [(g + a, g + b) for g in starts for a, b in pairs])

    across = within(quarters, [(0, 2), (1, 3), (2, 0), (3, 1)])
    below = within(quarters, [(0, 1), (1, 2), (2, 3)])
    above = within(quarters, [(1, 0), (2, 1), (3, 2)])
    passed = within(across, [(1, 0), (2, 3)])
    parts = (across, below, above, passed)
    place = (lax.axis_index("seq") % GROUP).astype(jnp.int32).reshape(1)
    own, *terms, steps = head_grads(
        place, key_tiles[0, 0], live_count[0, 0], saved_queries[0, 0].T, recv, parts, table
    )
    bias_share = lax.psum_scatter(bias_row_of(steps), "dp", scatter_dimension=1, tiled=True)

    def moved(x, d):
        pairs = [
            (a * sections + p + 1, b * sections + p)
            for a, b in passed_on(d)
            for p in range(sections - 1)
        ]
        return lax.ppermute(x, ("seq", "pipe"), pairs)

    terms = [moved(x, d) for d, x in enumerate(terms, 1)]
    own = moved(own, 0)
    packed = pl.pallas_call(
        sum_kernel,
        out_shape=jax.ShapeDtypeStruct((tiles_n, PACK, TILE), low),
        in_specs=[in_vmem] * GROUP,
        out_specs=in_vmem,
        compiler_params=params(16),
    )(own, *terms)
    back_in = lax.all_to_all(packed, "seq", split_axis=0, concat_axis=0, tiled=True)
    sent_query, sent_keys, sent_values = pl.pallas_call(
        unpack_kernel,
        out_shape=(
            jax.ShapeDtypeStruct((TILE, HEADS * HD), low),
            jax.ShapeDtypeStruct((TILE, KVH * HD), low),
            jax.ShapeDtypeStruct((TILE, KVH * HD), low),
        ),
        in_specs=[in_vmem],
        out_specs=(in_vmem,) * 3,
        compiler_params=params(16),
    )(back_in)
    return (
        sent_query[None, None],
        sent_keys[None, None],
        sent_values[None, None],
        bias_share[None],
    )


def solution(mesh):
    placed = (
        P("pipe", "dp", None, "seq"),
        P("pipe", "dp", "seq", None),
        P("pipe", "dp", "seq", None),
        P("pipe", "dp", "seq", None),
        P("pipe", "seq", None),
        P("pipe", "seq", None, None),
        P("pipe", "seq", None),
    )
    return jax.shard_map(
        per_device,
        mesh=mesh,
        in_specs=placed,
        out_specs=(
            P("pipe", "dp", "seq", None),
            P("pipe", "dp", "seq", None),
            P("pipe", "dp", "seq", None),
            P("pipe", "seq", "dp"),
        ),
        check_vma=False,
    )
```

```python
import jax
import jax.numpy as jnp
from jax import lax
from jax.experimental import pallas as pl
from jax.experimental.pallas import tpu as pltpu
from jax.sharding import PartitionSpec as P

HEADS = 32
KVH = 8
HD = 64
TILE = 128
BUCKET = 16
SLOTS = 4
GROUP = HEADS // KVH
QUART = TILE // GROUP
PACK = HD + QUART
ALONG = (2, 1, 3)

neg_big = -1e30
log2_e = 1.4426950408889634
low = jnp.bfloat16
wide = jnp.float32

in_vmem = pl.BlockSpec(memory_space=pltpu.VMEM)
in_smem = pl.BlockSpec(memory_space=pltpu.SMEM)


def params(mib):
    return pltpu.CompilerParams(vmem_limit_bytes=mib << 20)


def pack_kernel(grad_hbm, key_hbm, value_hbm, out_ref, grad_ref, key_ref, value_ref, sems):
    copies = [
        pltpu.make_async_copy(source, held, sems.at[n])
        for n, (source, held) in enumerate(
            ((grad_hbm, grad_ref), (key_hbm, key_ref), (value_hbm, value_ref))
        )
    ]
    for copy in copies:
        copy.start()
    copies[0].wait()
    for pair in range(HEADS // 2):
        turned = grad_ref[:, pair * 2 * HD : (pair + 1) * 2 * HD].T
        out_ref[2 * pair, 0:HD, :] = turned[0:HD]
        out_ref[2 * pair + 1, 0:HD, :] = turned[HD : 2 * HD]
    copies[1].wait()
    copies[2].wait()
    for g in range(KVH):
        both = jnp.concatenate(
            [key_ref[:, g * HD : (g + 1) * HD], value_ref[:, g * HD : (g + 1) * HD]], axis=1
        )
        for j in range(GROUP):
            out_ref[g * GROUP + j, HD:PACK, :] = both[j * QUART : (j + 1) * QUART]


def unpack_kernel(in_ref, query_ref, key_ref, value_ref):
    for pair in range(HEADS // 2):
        both = jnp.concatenate([in_ref[2 * pair, 0:HD, :], in_ref[2 * pair + 1, 0:HD, :]], axis=0)
        query_ref[:, pair * 2 * HD : (pair + 1) * 2 * HD] = both.T
    for pair in range(KVH // 2):
        sides = []
        for g in (2 * pair, 2 * pair + 1):
            sides.append(
                jnp.concatenate(
                    [in_ref[g * GROUP + j, HD:PACK, :] for j in range(GROUP)], axis=0
                )
            )
        at = slice(pair * 2 * HD, (pair + 1) * 2 * HD)
        key_ref[:, at] = jnp.concatenate([s[:, 0:HD] for s in sides], axis=1)
        value_ref[:, at] = jnp.concatenate([s[:, HD : 2 * HD] for s in sides], axis=1)


def sum_kernel(*refs):
    terms, own_ref, out_ref = refs[:-2], refs[-2], refs[-1]
    out_ref[:, 0:HD, :] = own_ref[:, 0:HD, :]
    total = own_ref[:, HD:PACK, :].astype(wide)
    for term in terms:
        total = total + term[...].astype(wide)
    out_ref[:, HD:PACK, :] = total.astype(low)


def table_kernel(steps_ref, table_ref):
    tiles_n = steps_ref.shape[0]
    for apart in range(tiles_n):
        near = steps_ref[apart : apart + 1, :]
        far = steps_ref[max(apart - 1, 0) : max(apart - 1, 0) + 1, :]
        line = jnp.broadcast_to(jnp.concatenate([near, far], axis=1) * log2_e, (TILE, 2 * TILE))
        turned = pltpu.roll(line, 0, 1, stride=1, stride_axis=0)[:, 0:TILE]
        if apart == 0:
            key_at = lax.broadcasted_iota(jnp.int32, (TILE, TILE), 0)
            query_at = lax.broadcasted_iota(jnp.int32, (TILE, TILE), 1)
            turned = jnp.where(key_at > query_at, neg_big, turned)
        table_ref[apart] = turned
    table_ref[tiles_n] = jnp.full((TILE, TILE), neg_big, wide)


def main_kernel(
    place_ref, tiles_ref, live_ref, query_ref, recv_ref, *refs,
):
    parts, table_ref, outs = refs[:GROUP], refs[GROUP], refs[GROUP + 1 : 2 * GROUP]
    own_ref, steps_ref = refs[2 * GROUP : 2 * GROUP + 2]
    kv, kt, acc, bias_acc, even, odd = refs[2 * GROUP + 2 :]
    tiles_n = recv_ref.shape[0]
    scale = HD ** (-0.5)
    place = place_ref[0]

    def quarter(j):
        return pl.ds(pl.multiple_of(lax.rem(j, GROUP) * QUART, QUART), QUART)

    def begin(b, carry):
        across, below, above, passed = [part[b] for part in parts]
        kv[b, quarter(place), :] = recv_ref[b, HD:PACK, :]
        kv[b, quarter(place + 2), :] = across
        kv[b, quarter(place + 3), :] = jnp.where(place == 0, passed, below)
        kv[b, quarter(place + 1), :] = jnp.where(place == GROUP - 1, passed, above)
        kt[b] = kv[b].T[0:HD]
        bias_acc[b] = jnp.zeros((TILE, TILE), wide)
        return carry

    lax.fori_loop(0, tiles_n, begin, 0, unroll=8)
    bias_acc[tiles_n] = jnp.zeros((TILE, TILE), wide)
    blank = jnp.zeros((HD, TILE), low)
    slots = [slice(s * TILE, (s + 1) * TILE) for s in range(SLOTS)]

    def weights_of(i):
        query = query_ref[:, pl.ds(pl.multiple_of(i * TILE, TILE), TILE)]
        return jnp.concatenate(
            [
                jnp.concatenate([query, blank], axis=1),
                jnp.concatenate([blank, recv_ref[i, 0:HD, :]], axis=1),
            ],
            axis=0,
        )

    def products(i):
        keys = jnp.concatenate([kv[tiles_ref[i, s]] for s in range(SLOTS)], axis=0)
        return jnp.dot(keys, weights_of(i), preferred_element_type=wide)

    def rest(i, both):
        live = live_ref[i]
        tile_at = [tiles_ref[i, s] for s in range(SLOTS)]
        apart = [jnp.where(s < live, i - tile_at[s], tiles_n) for s in range(SLOTS)]
        logits = [
            both[rows, 0:TILE] * (scale * log2_e) + table_ref[d] for rows, d in zip(slots, apart)
        ]
        most = jnp.maximum(jnp.maximum(logits[0], logits[1]), jnp.maximum(logits[2], logits[3]))
        top = jnp.max(most, axis=0, keepdims=True)
        raised, total, weighed = [], 0.0, 0.0
        for rows, logit in zip(slots, logits):
            raised.append(jnp.exp2(logit - top))
            total = total + raised[-1]
            weighed = weighed + raised[-1] * both[rows, TILE : 2 * TILE]
        inverse = 1.0 / jnp.sum(total, axis=0, keepdims=True)
        delta = jnp.sum(weighed, axis=0, keepdims=True) * inverse
        probs_low, grad_low = [], []
        for s in range(SLOTS):
            probs = raised[s] * inverse
            grad = probs * (both[slots[s], TILE : 2 * TILE] - delta)
            bias_acc[apart[s]] += grad
            probs_low.append(probs.astype(low))
            grad_low.append(grad.astype(low))
        grad_low = jnp.concatenate(grad_low, axis=0)
        probs_low = jnp.concatenate(probs_low, axis=0)
        terms = lax.dot_general(
            jnp.concatenate([grad_low, probs_low], axis=1),
            weights_of(i),
            (((1,), (1,)), ((), ())),
            preferred_element_type=wide,
        )
        keys_turned = jnp.concatenate([kt[t] for t in tile_at], axis=1)
        dq = jnp.dot(keys_turned, grad_low, preferred_element_type=wide)
        own_ref[i, 0:HD, :] = (dq * scale).astype(low)
        acc[i] = terms[slots[0]]
        for s in range(1, SLOTS):
            acc[tile_at[s]] += terms[slots[s]]

    even[...] = products(0)

    def two_tiles(n, carry):
        i = 2 * n
        odd[...] = products(i + 1)
        rest(i, even)
        even[...] = products(jnp.minimum(i + 2, tiles_n - 1))
        rest(i + 1, odd)
        return carry

    lax.fori_loop(0, tiles_n // 2, two_tiles, 0, unroll=4)
    lane = lax.broadcasted_iota(jnp.int32, (QUART, 2 * HD), 1)
    sizes = jnp.where(lane < HD, scale, 1.0)
    blank_right = jnp.zeros((TILE, TILE), wide)
    in_bucket = lax.broadcasted_iota(jnp.int32, (BUCKET, 2 * TILE), 1) % BUCKET
    before = in_bucket < lax.broadcasted_iota(jnp.int32, (BUCKET, 2 * TILE), 0)

    def end(b, carry):
        own_ref[b, HD:PACK, :] = (acc[b, quarter(place), :] * sizes).astype(low)
        for d, out in zip(ALONG, outs):
            out[b] = (acc[b, quarter(place + d), :] * sizes).astype(low)
        padded = jnp.concatenate([bias_acc[b], blank_right], axis=1)
        lined = padded[0:BUCKET]
        for step in range(1, TILE // BUCKET):
            rows = padded[step * BUCKET : (step + 1) * BUCKET]
            lined = lined + pltpu.roll(rows, 2 * TILE - step * BUCKET, 1)
        same = jnp.sum(jnp.where(before, 0.0, lined), axis=0, keepdims=True)
        less = jnp.sum(jnp.where(before, lined, 0.0), axis=0, keepdims=True)
        steps_ref[b] = same + pltpu.roll(less, 2 * TILE - BUCKET, 1)
        return carry

    lax.fori_loop(0, tiles_n, end, 0, unroll=8)


def make_table(bias_row, tiles_n):
    steps = jnp.repeat(bias_row.reshape(tiles_n, TILE // BUCKET), BUCKET, axis=1)
    return pl.pallas_call(
        table_kernel,
        out_shape=jax.ShapeDtypeStruct((tiles_n + 1, TILE, TILE), wide),
        in_specs=[in_vmem],
        out_specs=in_vmem,
        compiler_params=params(16),
    )(steps)


def head_grads(place, tile_list, live_slots, query, recv, parts, table):
    tiles_n = recv.shape[0]
    share = jax.ShapeDtypeStruct((tiles_n, QUART, 2 * HD), low)
    return pl.pallas_call(
        main_kernel,
        out_shape=(
            *[share] * (GROUP - 1),
            jax.ShapeDtypeStruct((tiles_n, PACK, TILE), low),
            jax.ShapeDtypeStruct((tiles_n, 1, 2 * TILE), wide),
        ),
        in_specs=[in_smem] * 3 + [in_vmem] * (GROUP + 3),
        out_specs=(in_vmem,) * (GROUP + 1),
        scratch_shapes=[
            pltpu.VMEM((tiles_n, TILE, 2 * HD), low),
            pltpu.VMEM((tiles_n, HD, TILE), low),
            pltpu.VMEM((tiles_n, TILE, 2 * HD), wide),
            pltpu.VMEM((tiles_n + 1, TILE, TILE), wide),
            pltpu.VMEM((SLOTS * TILE, 2 * TILE), wide),
            pltpu.VMEM((SLOTS * TILE, 2 * TILE), wide),
        ],
        compiler_params=params(32),
    )(place, tile_list, live_slots, query, recv, *parts, table)


def bias_row_of(steps):
    near, far = steps[:, 0, 0:TILE], steps[:, 0, TILE : 2 * TILE]
    far = jnp.concatenate([far[1:], jnp.zeros_like(far[:1])], axis=0)
    tiles_n = steps.shape[0]
    return (near + far).reshape(1, tiles_n * (TILE // BUCKET), BUCKET).sum(2)


def per_device(
    saved_queries, saved_keys, saved_values, output_grad, rel_bias, key_tiles, live_count
):
    seq_n, sections = lax.axis_size("seq"), lax.axis_size("pipe")
    tiles_n = key_tiles.shape[2]

    def passed_on(d):
        return [
            (g * GROUP + j, g * GROUP + (j + d) % GROUP)
            for g in range(seq_n // GROUP)
            for j in range(GROUP)
        ]

    def held(x):
        return pltpu.with_memory_space_constraint(x, pltpu.HBM)

    packed = pl.pallas_call(
        pack_kernel,
        out_shape=jax.ShapeDtypeStruct((HEADS, PACK, TILE), low),
        in_specs=[pl.BlockSpec(memory_space=pltpu.HBM)] * 3,
        out_specs=in_vmem,
        scratch_shapes=[
            pltpu.VMEM((TILE, HEADS * HD), low),
            pltpu.VMEM((TILE, KVH * HD), low),
            pltpu.VMEM((TILE, KVH * HD), low),
            pltpu.SemaphoreType.DMA((3,)),
        ],
        compiler_params=params(16),
    )(*[held(x[0, 0]) for x in (output_grad, saved_keys, saved_values)])
    recv = lax.all_to_all(packed, "seq", split_axis=0, concat_axis=0, tiled=True)
    table = make_table(rel_bias[0, 0], tiles_n)
    quarters, table = lax.optimization_barrier((recv[:, HD:PACK, :], table))
    starts = range(0, seq_n, GROUP)

    def within(x, pairs):
        return lax.ppermute(x, "seq", [(g + a, g + b) for g in starts for a, b in pairs])

    across = within(quarters, [(0, 2), (1, 3), (2, 0), (3, 1)])
    below = within(quarters, [(0, 1), (1, 2), (2, 3)])
    above = within(quarters, [(1, 0), (2, 1), (3, 2)])
    passed = within(across, [(1, 0), (2, 3)])
    parts = (across, below, above, passed)
    place = (lax.axis_index("seq") % GROUP).astype(jnp.int32).reshape(1)
    *terms, own, steps = head_grads(
        place, key_tiles[0, 0], live_count[0, 0], saved_queries[0, 0].T, recv, parts, table
    )
    bias_share = lax.psum_scatter(bias_row_of(steps), "dp", scatter_dimension=1, tiled=True)

    def moved(x, d):
        pairs = [
            (a * sections + p + 1, b * sections + p)
            for a, b in passed_on(d)
            for p in range(sections - 1)
        ]
        return lax.ppermute(x, ("seq", "pipe"), pairs)

    terms = [moved(x, d) for d, x in zip(ALONG, terms)]
    own = moved(own, 0)
    packed = pl.pallas_call(
        sum_kernel,
        out_shape=jax.ShapeDtypeStruct((tiles_n, PACK, TILE), low),
        in_specs=[in_vmem] * GROUP,
        out_specs=in_vmem,
        compiler_params=params(16),
    )(*terms, own)
    back_in = lax.all_to_all(packed, "seq", split_axis=0, concat_axis=0, tiled=True)
    sent_query, sent_keys, sent_values = pl.pallas_call(
        unpack_kernel,
        out_shape=(
            jax.ShapeDtypeStruct((TILE, HEADS * HD), low),
            jax.ShapeDtypeStruct((TILE, KVH * HD), low),
            jax.ShapeDtypeStruct((TILE, KVH * HD), low),
        ),
        in_specs=[in_vmem],
        out_specs=(in_vmem,) * 3,
        compiler_params=params(16),
    )(back_in)
    return (
        sent_query[None, None],
        sent_keys[None, None],
        sent_values[None, None],
        bias_share[None],
    )


def solution(mesh):
    placed = (
        P("pipe", "dp", None, "seq"),
        P("pipe", "dp", "seq", None),
        P("pipe", "dp", "seq", None),
        P("pipe", "dp", "seq", None),
        P("pipe", "seq", None),
        P("pipe", "seq", None, None),
        P("pipe", "seq", None),
    )
    return jax.shard_map(
        per_device,
        mesh=mesh,
        in_specs=placed,
        out_specs=(
            P("pipe", "dp", "seq", None),
            P("pipe", "dp", "seq", None),
            P("pipe", "dp", "seq", None),
            P("pipe", "seq", "dp"),
        ),
        check_vma=False,
    )
```
